32 devices in a mesh: tile: 8 (over y, x, core), plane: 4 (over z).
Axes of the slice: x: 2, y: 2, z: 4, core: 2. Of those that a mesh axis runs over, the one named last changes fastest.
Arguments:
- raw_tiles: bfloat16 [4, 64, 2, 16, 1024], P('plane', 'tile'), may hold values from 0.5 to 2.5
- flat_profile: bfloat16 [2, 16, 1024], P(None, 'plane'), may hold values from 0.5 to 1.5
- dark_profile: bfloat16 [2, 16, 1024], P(None, 'plane'), may hold values from 0 to 0.5
- destinations: int32 [4, 64, 1], P('plane', 'tile'), may hold values from 0 to 7, as said below
- positions: int32 [4, 64], P('plane', 'tile'), may hold values from 0 to 31
- levels: int32 [4, 64], P('plane', 'tile'), may hold values from 1 to 4
Outputs:
- stitched: bfloat16 [4, 2, 4096, 1024], P('plane', None, 'tile')
The draws below stay inside these ranges and needn't reach their ends.
Inputs may be any that keep to these rules, and one draw needn't show every extreme that they name: `destinations`: the owner of a tile acquired by the device at index i of tile (aligned blocks of 8 tiles of a plane) is one of i - 2, ..., i + 2 or i + 4, modulo 8; among one device's tiles no owner is named more than 2 times, some owner exactly 2 times, and the owner i + 4 exactly 2 times.
All inputs are finite; a program needn't handle non-finite values.
Results may differ from the reference program's by a relative error of at most 0.0045.
Values may be sent and summed in bfloat16 or wider, within the bound.
No kernel may reach another device: no remote copies, remote signals or barrier semaphores. Data moves between devices by JAX's collectives and lax.ppermute only.
A program may use at most 64 MiB of HBM per device.

```python
import jax
import jax.numpy as jnp
from jax import lax

W = 1024
CH = 2
TR = 16
CR = 512
NT = 8
CAP = 2
PLANES = 4
TILES = 64
N_TILE = 8
N_PLANE = 4


def draw_destinations(key, part):
    block_total = PLANES * N_TILE

    def one_block(block_key, block_id):
        key_full, key_mix, key_final = jax.random.split(block_key, 3)
        full_offset = jax.random.randint(key_full, (), 0, 5)
        base = jnp.repeat(jnp.arange(6, dtype=jnp.int32), CAP)
        mixed = base[jax.random.permutation(key_mix, 6 * CAP)]
        rank_key = jnp.where(mixed == full_offset, 0, jnp.where(mixed == 5, 1, 2)).astype(jnp.int32)
        order = jnp.argsort(rank_key, stable=True)
        chosen = mixed[order][:NT]
        chosen = jax.random.permutation(key_final, chosen)
        device_id = block_id % N_TILE
        step_to = jnp.where(chosen == 5, N_TILE // 2, chosen - 2)
        return ((device_id + step_to) % N_TILE).astype(jnp.int32)
    block_keys = jax.random.split(jax.random.fold_in(key, 71), block_total)
    owners = jax.vmap(one_block)(block_keys, jnp.arange(block_total, dtype=jnp.int32))
    return owners.reshape(PLANES, N_TILE * NT, 1).astype(jnp.int32)


def place_ends(entries, rng, smallest, largest):
    shape = entries.shape
    index_at = [jax.random.randint(jax.random.fold_in(rng, axis), (), 0, shape[axis]) for axis in range(len(shape))]
    entries = entries.at[tuple(index_at)].set(smallest)
    longest = shape.index(max(shape))
    index_at[longest] = (index_at[longest] + 1) % shape[longest]
    return entries.at[tuple(index_at)].set(largest)


def block_levels(rng, extent, cuts, low, largest):
    loudness = 1.0
    for position, shards_of in cuts:
        draws = jax.random.uniform(jax.random.fold_in(jax.random.fold_in(rng, 6), position), (shards_of,), jnp.float32, low / len(cuts), largest / len(cuts))
        loudness = loudness * jnp.repeat(jnp.exp(draws), extent[position] // shards_of).reshape((-1,) + (1,) * (len(extent) - 1 - position))
    return loudness


def setup_inputs(seed: int = 0) -> dict:
    arg_keys = jax.random.split(jax.random.key(seed), 7)
    raw_tiles = jnp.clip(0.5 + 2.0 * jax.random.uniform(arg_keys[0], (PLANES, TILES, CH, TR, W), jnp.float32) ** block_levels(arg_keys[0], (PLANES, TILES, CH, TR, W), ((0, 4), (1, 8)), -0.2, 0.2), 0.5, 2.5).astype(jnp.bfloat16)
    flat_profile = jnp.clip(0.5 + 1.0 * jax.random.uniform(arg_keys[1], (CH, TR, W), jnp.float32) ** block_levels(arg_keys[1], (CH, TR, W), ((1, 4),), -0.2, 0.2), 0.5, 1.5).astype(jnp.bfloat16)
    dark_profile = jnp.clip(0.5 * jax.random.uniform(arg_keys[2], (CH, TR, W), jnp.float32) ** block_levels(arg_keys[2], (CH, TR, W), ((1, 4),), -0.2, 0.2), 0.0, 0.5).astype(jnp.bfloat16)
    destinations = draw_destinations(jax.random.fold_in(arg_keys[6], 71), 0)
    positions = place_ends(jax.random.randint(arg_keys[4], (PLANES, TILES), 0, (CR - TR) // 16 + 1), jax.random.fold_in(arg_keys[4], 1), 0, ((CR - TR) // 16 + 1) - 1).astype(jnp.int32)
    levels = place_ends(jax.random.randint(arg_keys[5], (PLANES, TILES), 1, 5), jax.random.fold_in(arg_keys[5], 1), 1, 4).astype(jnp.int32)
    return {"raw_tiles": raw_tiles, "flat_profile": flat_profile, "dark_profile": dark_profile, "destinations": destinations, "positions": positions, "levels": levels}


screen_weight = 0.5


def ramp_weights():
    tile_row = jnp.arange(TR)
    return jnp.minimum(tile_row + 1, TR - tile_row).astype(jnp.float32)


def apply_weights(camera, flat_full, dark_full, gains):
    corrected = (camera.astype(jnp.float32) - dark_full.astype(jnp.float32)) / flat_full.astype(jnp.float32)
    scale = gains * ramp_weights()[:, None]
    return (corrected * scale).astype(jnp.bfloat16)


def smooth_sweep(field, blended):
    padded = jnp.pad(field, ((0, 0), (1, 1), (1, 1)))
    neighbours = padded[:, :-2, 1:-1] + padded[:, 2:, 1:-1] + padded[:, 1:-1, :-2] + padded[:, 1:-1, 2:]
    return (screen_weight * blended + neighbours) / (screen_weight + 4.0)


def stitch_plane(camera, owners, grid_pos, gains, flat_profile, dark_profile):
    anchor = jnp.zeros((), jnp.int32)

    def add_tile(state_pair, record):
        accumulated, weight_sum = state_pair
        one_tile, owner, offset, gain = record
        first_row = (owner * CR + 16 * offset).astype(jnp.int32)
        weighted = apply_weights(one_tile, flat_profile, dark_profile, gain.astype(jnp.float32)).astype(jnp.float32)
        current = lax.dynamic_slice(accumulated, (anchor, first_row, anchor), (CH, TR, W))
        accumulated = lax.dynamic_update_slice(accumulated, current + weighted, (anchor, first_row, anchor))
        current_w = lax.dynamic_slice(weight_sum, (first_row,), (TR,))
        weight_sum = lax.dynamic_update_slice(weight_sum, current_w + gain.astype(jnp.float32) * ramp_weights(), (first_row,))
        return (accumulated, weight_sum), None

    start_pair = (jnp.zeros((CH, N_TILE * CR, W), jnp.float32), jnp.zeros((N_TILE * CR,), jnp.float32))
    (accumulated, weight_sum), _ = lax.scan(add_tile, start_pair, (camera, owners[:, 0], grid_pos, gains))
    blended = accumulated / jnp.maximum(weight_sum, 1.0)[None, :, None]
    field = blended
    for sweep_id in range(3):
        field = smooth_sweep(field, blended)
    return field.astype(jnp.bfloat16)


def reference(raw_tiles, flat_profile, dark_profile, destinations, positions, levels):
    planes_out = []
    for plane_id in range(N_PLANE):
        planes_out.append(stitch_plane(raw_tiles[plane_id], destinations[plane_id], positions[plane_id], levels[plane_id], flat_profile, dark_profile))
    return jnp.stack(planes_out, 0)
```

```python
import functools

import jax
import jax.numpy as jnp
from jax import lax
from jax.experimental import pallas as pl
from jax.experimental.pallas import tpu as pltpu
from jax.sharding import PartitionSpec as P

CR = 512
CAP = 2
screen_weight = 0.5


_D = screen_weight + 4.0
c0 = screen_weight / _D
c1 = screen_weight / _D**2
c2 = screen_weight / _D**3
c3 = 1.0 / _D**3
TAPS = (
    (c0 + 2 * c2, c1 + 3 * c3, c2, c3),
    (c1 + 6 * c3, 2 * c2, 3 * c3, 0.0),
    (c2, 3 * c3, 0.0, 0.0),
    (c3, 0.0, 0.0, 0.0),
)


def steps_of(count):
    return (0, 1, 2, count - 1, count - 2, count // 2)


def pack_kernel(count, dest, pos, lev, cam, flat, dark, *rest):
    outs = rest[:-4]
    prof, idx, lv, ps = rest[-4:]
    steps = steps_of(count)
    classes = len(steps)
    me = lax.axis_index("tile")
    tiles, channels, rows, width = cam.shape[1:]
    for s in range(classes * CAP):
        idx[s] = 0
        lv[s] = 0
        ps[s] = 0
    owners = [dest[0, t, 0] for t in range(tiles)]
    for t in range(tiles):
        off = owners[t] - me
        off = jnp.where(off < 0, off + count, off)
        cls = jnp.int32(0)
        for k, step in enumerate(steps):
            cls = jnp.where(off == step, k, cls)
        rank = jnp.int32(0)
        for u in range(t):
            rank = rank + (owners[u] == owners[t]).astype(jnp.int32)
        slot = cls * CAP + jnp.minimum(rank, CAP - 1)
        idx[slot] = t
        lv[slot] = lev[0, t]
        ps[slot] = pos[0, t]
    pieces = [flat[0], flat[1], dark[0], dark[1]]
    prof[...] = jnp.concatenate([p.astype(jnp.float32) for p in pieces], 0).astype(jnp.bfloat16)
    row = lax.broadcasted_iota(jnp.int32, (16, 128), 0)
    lane = lax.broadcasted_iota(jnp.int32, (16, 128), 1)
    second = (lane // 16) % 2 == 1
    for k in range(classes):
        out = outs[k]
        for j in range(CAP):
            t = idx[k * CAP + j]
            for c in range(channels):
                for b in range(width // 128):
                    at = ((c * CAP + j) * (width // 128) + b) * rows
                    out[at : at + rows, :] = cam[0, t, c, :, b * 128 : (b + 1) * 128]
        p0, p1 = ps[k * CAP].astype(jnp.float32), ps[k * CAP + 1].astype(jnp.float32)
        l0, l1 = lv[k * CAP].astype(jnp.float32), lv[k * CAP + 1].astype(jnp.float32)
        info = jnp.where(second, p1, p0)
        info = jnp.where(row == 1, jnp.where(second, l1, l0), info)
        info = jnp.where(row == 2, p0, info)
        info = jnp.where(row == 3, p1, info)
        info = jnp.where(row == 4, l0, info)
        info = jnp.where(row == 5, l1, info)
        end = channels * CAP * (width // 128) * rows
        out[end : end + 16, :] = info.astype(jnp.bfloat16)


def profile_kernel(planes, rows, own, *rest):
    others = rest[:-2]
    rflat, darkf = rest[-2:]
    here = lax.axis_index("plane")
    held = [own[...].astype(jnp.float32)] + [o[...].astype(jnp.float32) for o in others]
    part = rows // planes
    blocks = []
    for q in range(planes):
        back = here - q
        back = jnp.where(back < 0, back + planes, back)
        piece = held[0]
        for s in range(1, planes):
            piece = jnp.where(back == s, held[s], piece)
        blocks.append(piece)
    for c in range(2):
        flat = jnp.concatenate([b[c * part : (c + 1) * part] for b in blocks], 0)
        rflat[c] = 1.0 / flat
        darkf[c] = jnp.concatenate([b[(2 + c) * part : (3 + c) * part] for b in blocks], 0)


def read_slots(pays, end):
    pos, lev, infos = [], [], []
    for p in pays:
        info = p[end : end + 16, :].astype(jnp.float32)
        infos.append(info)
        pos += [info[2:3], info[3:4]]
        lev += [info[4:5], info[5:6]]
    return pos, lev, infos


def total_level(where, pos, lev):
    total = jnp.zeros_like(where)
    for p, v in zip(pos, lev):
        total = total + jnp.where(where == p, v, 0.0)
    return total


def strip_kernel(last, width, *refs):
    pays, (rflat, darkf, top, bot) = refs[:-4], refs[-4:]
    blocks = width // 128
    rows = 16
    end = pays[0].shape[0] - 16
    pos, lev, _ = read_slots(pays, end)
    sub = lax.broadcasted_iota(jnp.int32, (8, 128), 0)
    rise = (sub + 1).astype(jnp.float32)
    fall = (8 - sub).astype(jnp.float32)
    gains_top, gains_bot = [], []
    for p, v in zip(pos, lev):
        total = total_level(p, pos, lev)
        gains_top.append(jnp.where(p == 0.0, v, 0.0) * rise / jnp.maximum(total * rise, 1.0))
        gains_bot.append(jnp.where(p == last, v, 0.0) * fall / jnp.maximum(total * fall, 1.0))
    for c in range(2):
        for b in range(blocks):
            cols = slice(b * 128, (b + 1) * 128)
            dk, rf = darkf[c, :, cols], rflat[c, :, cols]
            high = jnp.zeros((8, 128), jnp.float32)
            low = jnp.zeros((8, 128), jnp.float32)
            for s in range(len(pos)):
                at = ((c * CAP + s % CAP) * blocks + b) * rows
                raw = pays[s // CAP][at : at + rows, :].astype(jnp.float32)
                corrected = (raw - dk) * rf
                high = high + gains_top[s] * corrected[:8]
                low = low + gains_bot[s] * corrected[8:]
            top[c * 8 : (c + 1) * 8, cols] = high.astype(jnp.bfloat16)
            bot[c * 8 : (c + 1) * 8, cols] = low.astype(jnp.bfloat16)


def shift_sum(h):
    width = h.shape[1]
    lane = lax.broadcasted_iota(jnp.int32, h.shape, 1)
    left = jnp.where(lane == 0, 0.0, pltpu.roll(h, 1, 1))
    right = jnp.where(lane == width - 1, 0.0, pltpu.roll(h, width - 1, 1))
    return left + right


def main_kernel(width, *refs):
    pays, (rflat, darkf, out, edges, coef, hall) = refs[:-6], refs[-6:]
    blocks = width // 128
    rows = 16
    canvas = out.shape[2]
    end = pays[0].shape[0] - 16
    c = pl.program_id(0)

    @pl.when(c == 0)
    def _():
        pos, lev, infos = read_slots(pays, end)
        lane = lax.broadcasted_iota(jnp.int32, (1, 128), 1)
        r = (lane % 16).astype(jnp.float32)
        ramp = jnp.minimum(r + 1.0, 16.0 - r)
        power = lane // 32
        y = lax.broadcasted_iota(jnp.int32, (canvas, 128), 0).astype(jnp.float32)
        for k in range(len(pays)):
            here, level = infos[k][0:1], infos[k][1:2]
            gain = level * ramp / jnp.maximum(total_level(here, pos, lev) * ramp, 1.0)
            taps = []
            for d in range(4):
                tap = jnp.full((1, 128), TAPS[0][d], jnp.float32)
                for j in range(1, 4):
                    tap = jnp.where(power == j, TAPS[j][d], tap)
                taps.append(tap * gain)
            dist = jnp.abs(y - (here * 16.0 + r))
            value = jnp.where(dist == 0.0, taps[0], 0.0)
            for d in range(1, 4):
                value = jnp.where(dist == float(d), taps[d], value)
            coef[:, k * 128 : (k + 1) * 128] = value.astype(jnp.bfloat16)

    dk, rf = darkf[c], rflat[c]
    for k in range(len(pays)):
        for s in range(CAP):
            pieces = []
            for b in range(blocks):
                at = pl.multiple_of(c * (CAP * blocks * rows), 16) + (s * blocks + b) * rows
                pieces.append(pays[k][pl.ds(at, rows), :].astype(jnp.float32))
            h = (jnp.concatenate(pieces, 1) - dk) * rf
            for j in range(4):
                if j:
                    h = shift_sum(h)
                at = k * 128 + j * 32 + s * 16
                hall[at : at + 16, :] = h.astype(jnp.bfloat16)
    field = jnp.dot(coef[...], hall[...], preferred_element_type=jnp.float32)
    out[0, 0] = field.astype(jnp.bfloat16)
    edges[0, 0:8] = field[0:8]
    edges[0, 8:16] = field[canvas - 8 : canvas]


def edge_kernel(count, field, edges, above, below, top, bot, out, buf, sems, done):
    me = lax.axis_index("tile")
    canvas = field.shape[2]
    places = [(c, e) for c in range(2) for e in range(2)]
    reads = []
    for n, (c, e) in enumerate(places):
        span = pl.ds(0 if e == 0 else canvas - 16, 16)
        reads.append(pltpu.make_async_copy(field.at[0, c, span, :], buf.at[n], sems.at[n]))
    for r in reads:
        r.start()
    width = edges.shape[2]
    sub = lax.broadcasted_iota(jnp.int32, (8, width), 0)
    merged = []
    for c, e in places:
        rows = slice(c * 8, (c + 1) * 8)
        if e == 0:
            halo = above[rows].astype(jnp.float32)
            own = top[rows].astype(jnp.float32)
            image = jnp.where(sub == 6, -pltpu.roll(own, 6, 0), jnp.where(sub == 5, -pltpu.roll(own, 4, 0), 0.0))
            halo = jnp.where(me == 0, image, halo)
            halo = jnp.where(sub >= 5, halo, 0.0)
        else:
            halo = below[rows].astype(jnp.float32)
            own = bot[rows].astype(jnp.float32)
            image = jnp.where(sub == 1, -pltpu.roll(own, 2, 0), jnp.where(sub == 2, -pltpu.roll(own, 4, 0), 0.0))
            halo = jnp.where(me == count - 1, image, halo)
            halo = jnp.where(sub <= 2, halo, 0.0)
        h1 = shift_sum(halo)
        h2 = shift_sum(h1)
        near = TAPS[0][1] * halo + TAPS[1][1] * h1 + TAPS[2][1] * h2
        mid = TAPS[0][2] * halo + TAPS[1][2] * h1
        far = TAPS[0][3] * halo
        total = edges[c, e * 8 : (e + 1) * 8, :]
        for d, part in ((1, near), (2, mid), (3, far)):
            if e == 0:
                total = total + jnp.where(sub < d, pltpu.roll(part, d, 0), 0.0)
            else:
                total = total + jnp.where(sub >= 8 - d, pltpu.roll(part, 8 - d, 0), 0.0)
        merged.append(total)
    writes = []
    for n, (c, e) in enumerate(places):
        reads[n].wait()
        old = buf[n].astype(jnp.float32)
        parts = [merged[n], old[8:]] if e == 0 else [old[:8], merged[n]]
        buf[n] = jnp.concatenate(parts, 0).astype(jnp.bfloat16)
        span = pl.ds(0 if e == 0 else canvas - 16, 16)
        write = pltpu.make_async_copy(buf.at[n], out.at[0, c, span, :], done.at[n])
        write.start()
        writes.append(write)
    for w in writes:
        w.wait()


def vmem():
    return pl.BlockSpec(memory_space=pltpu.VMEM)


def smem():
    return pl.BlockSpec(memory_space=pltpu.SMEM)


def per_device(raw_tiles, flat_profile, dark_profile, destinations, positions, levels):
    count = lax.axis_size("tile")
    planes = lax.axis_size("plane")
    _, tiles, channels, rows, width = raw_tiles.shape
    steps = steps_of(count)
    classes = len(steps)
    length = channels * CAP * rows * (width // 128)
    payload = jax.ShapeDtypeStruct((length + 16, 128), jnp.bfloat16)
    part = flat_profile.shape[1]
    profile = jax.ShapeDtypeStruct((4 * part, width), jnp.bfloat16)
    slots = classes * CAP
    packed = pl.pallas_call(
        functools.partial(pack_kernel, count),
        out_shape=[payload] * classes + [profile],
        in_specs=[smem(), smem(), smem(), vmem(), vmem(), vmem()],
        out_specs=[vmem()] * (classes + 1),
        scratch_shapes=[pltpu.SMEM((slots,), jnp.int32)] * 3,
        name="pack",
    )(destinations, positions, levels, raw_tiles, flat_profile, dark_profile)
    own = packed[-1]
    others = [
        lax.ppermute(own, "plane", [(i, (i + s) % planes) for i in range(planes)]) for s in range(1, planes)
    ]
    pays = [packed[0]] + [
        lax.ppermute(packed[k], "tile", [(i, (i + steps[k]) % count) for i in range(count)])
        for k in range(1, classes)
    ]
    full = jax.ShapeDtypeStruct((channels, rows, width), jnp.float32)
    rflat, darkf = pl.pallas_call(
        functools.partial(profile_kernel, planes, rows),
        out_shape=[full, full],
        in_specs=[vmem()] * planes,
        out_specs=[vmem()] * 2,
        name="profile",
    )(own, *others)
    strip = jax.ShapeDtypeStruct((channels * 8, width), jnp.bfloat16)
    top, bot = pl.pallas_call(
        functools.partial(strip_kernel, float(CR // rows - 1), width),
        out_shape=[strip, strip],
        in_specs=[vmem()] * (classes + 2),
        out_specs=[vmem()] * 2,
        name="strips",
    )(*pays, rflat, darkf)
    above = lax.ppermute(bot, "tile", [(i, i + 1) for i in range(count - 1)])
    below = lax.ppermute(top, "tile", [(i + 1, i) for i in range(count - 1)])
    field, edges = pl.pallas_call(
        functools.partial(main_kernel, width),
        grid=(channels,),
        out_shape=[
            jax.ShapeDtypeStruct((1, channels, CR, width), jnp.bfloat16),
            jax.ShapeDtypeStruct((channels, 16, width), jnp.float32),
        ],
        in_specs=[vmem()] * (classes + 2),
        out_specs=[
            pl.BlockSpec((1, 1, CR, width), lambda c: (0, c, 0, 0)),
            pl.BlockSpec((1, 16, width), lambda c: (c, 0, 0)),
        ],
        scratch_shapes=[
            pltpu.VMEM((CR, classes * 128), jnp.bfloat16),
            pltpu.VMEM((classes * 128, width), jnp.bfloat16),
        ],
        name="place",
    )(*pays, rflat, darkf)
    return pl.pallas_call(
        functools.partial(edge_kernel, count),
        out_shape=jax.ShapeDtypeStruct(field.shape, field.dtype),
        in_specs=[pl.BlockSpec(memory_space=pl.ANY)] + [vmem()] * 5,
        out_specs=pl.BlockSpec(memory_space=pl.ANY),
        scratch_shapes=[
            pltpu.VMEM((4, 16, width), jnp.bfloat16),
            pltpu.SemaphoreType.DMA((4,)),
            pltpu.SemaphoreType.DMA((4,)),
        ],
        input_output_aliases={0: 0},
        name="edge",
    )(field, edges, above, below, top, bot)


def solution(mesh):
    placed = (
        P("plane", "tile", None, None, None),
        P(None, "plane", None),
        P(None, "plane", None),
        P("plane", "tile", None),
        P("plane", "tile"),
        P("plane", "tile"),
    )
    return jax.shard_map(
        per_device,
        mesh=mesh,
        in_specs=placed,
        out_specs=P("plane", None, "tile", None),
        check_vma=False,
    )
```

```python
import functools

import jax
import jax.numpy as jnp
from jax import lax
from jax.experimental import pallas as pl
from jax.experimental.pallas import tpu as pltpu
from jax.sharding import PartitionSpec as P


CR = 512
CAP = 2
screen_weight = 0.5


_D = screen_weight + 4.0
c0 = screen_weight / _D
c1 = screen_weight / _D**2
c2 = screen_weight / _D**3
c3 = 1.0 / _D**3
TAPS = (
    (c0 + 2 * c2, c1 + 3 * c3, c2, c3),
    (c1 + 6 * c3, 2 * c2, 3 * c3, 0.0),
    (c2, 3 * c3, 0.0, 0.0),
    (c3, 0.0, 0.0, 0.0),
)


def steps_of(count):
    return (0, 1, 2, count - 1, count - 2, count // 2)


def pack_kernel(count, dest_in, pos_in, lev_in, cam_in, flat_in, dark_in, *rest):
    outs = rest[:-11]
    prof, dest, pos, lev, cam, flat, dark, idx, lv, ps, sems = rest[-11:]
    moves = [(dest_in, dest), (pos_in, pos), (lev_in, lev), (flat_in, flat), (dark_in, dark), (cam_in, cam)]
    copies = [pltpu.make_async_copy(src, dst, sems.at[n]) for n, (src, dst) in enumerate(moves)]
    for copy in copies:
        copy.start()
    steps = steps_of(count)
    classes = len(steps)
    me = lax.axis_index("tile")
    tiles, channels, rows, width = cam.shape[1:]
    for s in range(classes * CAP):
        idx[s] = 0
        lv[s] = 0
        ps[s] = 0
    for copy in copies[:3]:
        copy.wait()
    owners = [dest[0, t] for t in range(tiles)]
    for t in range(tiles):
        off = owners[t] - me
        off = jnp.where(off < 0, off + count, off)
        cls = jnp.int32(0)
        for k, step in enumerate(steps):
            cls = jnp.where(off == step, k, cls)
        rank = jnp.int32(0)
        for u in range(t):
            rank = rank + (owners[u] == owners[t]).astype(jnp.int32)
        slot = cls * CAP + jnp.minimum(rank, CAP - 1)
        idx[slot] = t
        lv[slot] = lev[0, t]
        ps[slot] = pos[0, t]
    copies[3].wait()
    copies[4].wait()
    pieces = [flat[0], flat[1], dark[0], dark[1]]
    prof[...] = jnp.concatenate([p.astype(jnp.float32) for p in pieces], 0).astype(jnp.bfloat16)
    row = lax.broadcasted_iota(jnp.int32, (16, 128), 0)
    lane = lax.broadcasted_iota(jnp.int32, (16, 128), 1)
    second = (lane // 16) % 2 == 1
    copies[5].wait()
    for k in range(classes):
        out = outs[k]
        for j in range(CAP):
            t = idx[k * CAP + j]
            for c in range(channels):
                for b in range(width // 128):
                    at = ((c * CAP + j) * (width // 128) + b) * rows
                    out[at : at + rows, :] = cam[0, t, c, :, b * 128 : (b + 1) * 128]
        p0, p1 = ps[k * CAP].astype(jnp.float32), ps[k * CAP + 1].astype(jnp.float32)
        l0, l1 = lv[k * CAP].astype(jnp.float32), lv[k * CAP + 1].astype(jnp.float32)
        info = jnp.where(second, p1, p0)
        info = jnp.where(row == 1, jnp.where(second, l1, l0), info)
        info = jnp.where(row == 2, p0, info)
        info = jnp.where(row == 3, p1, info)
        info = jnp.where(row == 4, l0, info)
        info = jnp.where(row == 5, l1, info)
        end = channels * CAP * (width // 128) * rows
        out[end : end + 16, :] = info.astype(jnp.bfloat16)


def profile_kernel(planes, rows, own, *rest):
    others = rest[:-2]
    rflat, darkf = rest[-2:]
    here = lax.axis_index("plane")
    held = [own[...].astype(jnp.float32)] + [o[...].astype(jnp.float32) for o in others]
    part = rows // planes
    blocks = []
    for q in range(planes):
        back = here - q
        back = jnp.where(back < 0, back + planes, back)
        piece = held[0]
        for s in range(1, planes):
            piece = jnp.where(back == s, held[s], piece)
        blocks.append(piece)
    for c in range(2):
        flat = jnp.concatenate([b[c * part : (c + 1) * part] for b in blocks], 0)
        rflat[c] = 1.0 / flat
        darkf[c] = jnp.concatenate([b[(2 + c) * part : (3 + c) * part] for b in blocks], 0)


def read_slots(pays, end):
    pos, lev, infos = [], [], []
    for p in pays:
        info = p[end : end + 16, :].astype(jnp.float32)
        infos.append(info)
        pos += [info[2:3], info[3:4]]
        lev += [info[4:5], info[5:6]]
    return pos, lev, infos


def total_level(where, pos, lev):
    total = jnp.zeros_like(where)
    for p, v in zip(pos, lev):
        total = total + jnp.where(where == p, v, 0.0)
    return total


def strip_kernel(last, width, *refs):
    pays, (rflat, darkf, top, bot) = refs[:-4], refs[-4:]
    blocks = width // 128
    rows = 16
    end = pays[0].shape[0] - 16
    pos, lev, _ = read_slots(pays, end)
    sub = lax.broadcasted_iota(jnp.int32, (8, 128), 0)
    rise = (sub + 1).astype(jnp.float32)
    fall = (8 - sub).astype(jnp.float32)
    gains_top, gains_bot = [], []
    for p, v in zip(pos, lev):
        total = total_level(p, pos, lev)
        gains_top.append(jnp.where(p == 0.0, v, 0.0) * rise / jnp.maximum(total * rise, 1.0))
        gains_bot.append(jnp.where(p == last, v, 0.0) * fall / jnp.maximum(total * fall, 1.0))
    for c in range(2):
        for b in range(blocks):
            cols = slice(b * 128, (b + 1) * 128)
            dk, rf = darkf[c, :, cols], rflat[c, :, cols]
            high = jnp.zeros((8, 128), jnp.float32)
            low = jnp.zeros((8, 128), jnp.float32)
            for s in range(len(pos)):
                at = ((c * CAP + s % CAP) * blocks + b) * rows
                raw = pays[s // CAP][at : at + rows, :].astype(jnp.float32)
                corrected = (raw - dk) * rf
                high = high + gains_top[s] * corrected[:8]
                low = low + gains_bot[s] * corrected[8:]
            top[c * 8 : (c + 1) * 8, cols] = high.astype(jnp.bfloat16)
            bot[c * 8 : (c + 1) * 8, cols] = low.astype(jnp.bfloat16)


def shift_sum(h):
    width = h.shape[1]
    lane = lax.broadcasted_iota(jnp.int32, h.shape, 1)
    left = jnp.where(lane == 0, 0.0, pltpu.roll(h, 1, 1))
    right = jnp.where(lane == width - 1, 0.0, pltpu.roll(h, width - 1, 1))
    return left + right


def main_kernel(width, *refs):
    pays, (rflat, darkf, out, edges, coef, hall) = refs[:-6], refs[-6:]
    blocks = width // 128
    rows = 16
    canvas = out.shape[2]
    end = pays[0].shape[0] - 16
    c = pl.program_id(0)

    @pl.when(c == 0)
    def _():
        pos, lev, infos = read_slots(pays, end)
        lane = lax.broadcasted_iota(jnp.int32, (1, 128), 1)
        r = (lane % 16).astype(jnp.float32)
        ramp = jnp.minimum(r + 1.0, 16.0 - r)
        power = lane // 32
        y = lax.broadcasted_iota(jnp.int32, (canvas, 128), 0).astype(jnp.float32)
        for k in range(len(pays)):
            here, level = infos[k][0:1], infos[k][1:2]
            gain = level * ramp / jnp.maximum(total_level(here, pos, lev) * ramp, 1.0)
            taps = []
            for d in range(4):
                tap = jnp.full((1, 128), TAPS[0][d], jnp.float32)
                for j in range(1, 4):
                    tap = jnp.where(power == j, TAPS[j][d], tap)
                taps.append(tap * gain)
            dist = jnp.abs(y - (here * 16.0 + r))
            value = jnp.where(dist == 0.0, taps[0], 0.0)
            for d in range(1, 4):
                value = jnp.where(dist == float(d), taps[d], value)
            coef[:, k * 128 : (k + 1) * 128] = value.astype(jnp.bfloat16)

    dk, rf = darkf[c], rflat[c]
    for k in range(len(pays)):
        for s in range(CAP):
            pieces = []
            for b in range(blocks):
                at = pl.multiple_of(c * (CAP * blocks * rows), 16) + (s * blocks + b) * rows
                pieces.append(pays[k][pl.ds(at, rows), :].astype(jnp.float32))
            h = (jnp.concatenate(pieces, 1) - dk) * rf
            for j in range(4):
                if j:
                    h = shift_sum(h)
                at = k * 128 + j * 32 + s * 16
                hall[at : at + 16, :] = h.astype(jnp.bfloat16)
    field = jnp.dot(coef[...], hall[...], preferred_element_type=jnp.float32)
    out[0, 0] = field.astype(jnp.bfloat16)
    edges[c, 0:8] = field[0:8]
    edges[c, 8:16] = field[canvas - 8 : canvas]


def edge_kernel(count, field, edges, above, below, top, bot, out, buf, sems, done):
    me = lax.axis_index("tile")
    canvas = field.shape[2]
    places = [(c, e) for c in range(2) for e in range(2)]
    reads = []
    for n, (c, e) in enumerate(places):
        span = pl.ds(0 if e == 0 else canvas - 16, 16)
        reads.append(pltpu.make_async_copy(field.at[0, c, span, :], buf.at[n], sems.at[n]))
    for r in reads:
        r.start()
    width = edges.shape[2]
    sub = lax.broadcasted_iota(jnp.int32, (8, width), 0)
    merged = []
    for c, e in places:
        rows = slice(c * 8, (c + 1) * 8)
        if e == 0:
            halo = above[rows].astype(jnp.float32)
            own = top[rows].astype(jnp.float32)
            image = jnp.where(sub == 6, -pltpu.roll(own, 6, 0), jnp.where(sub == 5, -pltpu.roll(own, 4, 0), 0.0))
            halo = jnp.where(me == 0, image, halo)
            halo = jnp.where(sub >= 5, halo, 0.0)
        else:
            halo = below[rows].astype(jnp.float32)
            own = bot[rows].astype(jnp.float32)
            image = jnp.where(sub == 1, -pltpu.roll(own, 2, 0), jnp.where(sub == 2, -pltpu.roll(own, 4, 0), 0.0))
            halo = jnp.where(me == count - 1, image, halo)
            halo = jnp.where(sub <= 2, halo, 0.0)
        h1 = shift_sum(halo)
        h2 = shift_sum(h1)
        near = TAPS[0][1] * halo + TAPS[1][1] * h1 + TAPS[2][1] * h2
        mid = TAPS[0][2] * halo + TAPS[1][2] * h1
        far = TAPS[0][3] * halo
        total = edges[c, e * 8 : (e + 1) * 8, :]
        for d, part in ((1, near), (2, mid), (3, far)):
            if e == 0:
                total = total + jnp.where(sub < d, pltpu.roll(part, d, 0), 0.0)
            else:
                total = total + jnp.where(sub >= 8 - d, pltpu.roll(part, 8 - d, 0), 0.0)
        merged.append(total)
    writes = []
    for n, (c, e) in enumerate(places):
        reads[n].wait()
        old = buf[n].astype(jnp.float32)
        parts = [merged[n], old[8:]] if e == 0 else [old[:8], merged[n]]
        buf[n] = jnp.concatenate(parts, 0).astype(jnp.bfloat16)
        span = pl.ds(0 if e == 0 else canvas - 16, 16)
        write = pltpu.make_async_copy(buf.at[n], out.at[0, c, span, :], done.at[n])
        write.start()
        writes.append(write)
    for w in writes:
        w.wait()


def vmem():
    return pl.BlockSpec(memory_space=pltpu.VMEM)


def resident(*arrays):
    return [pltpu.with_memory_space_constraint(a, pltpu.VMEM) for a in arrays]


def grant(mib):
    return pltpu.CompilerParams(vmem_limit_bytes=mib << 20)


ORDER = (4, 2, 5, 3, 1)


def stitch(raw_tiles, flat_profile, dark_profile, destinations, positions, levels):
    count = lax.axis_size("tile")
    planes = lax.axis_size("plane")
    _, tiles, channels, rows, width = raw_tiles.shape
    steps = steps_of(count)
    classes = len(steps)
    length = channels * CAP * rows * (width // 128)
    payload = pltpu.VMEM((length + 16, 128), jnp.bfloat16)
    part = flat_profile.shape[1]
    profile = pltpu.VMEM((4 * part, width), jnp.bfloat16)
    slots = classes * CAP
    packed = pl.pallas_call(
        functools.partial(pack_kernel, count),
        out_shape=[payload] * classes + [profile],
        in_specs=[pl.BlockSpec(memory_space=pltpu.HBM)] * 6,
        out_specs=[vmem()] * (classes + 1),
        scratch_shapes=[pltpu.SMEM((1, tiles), jnp.int32)] * 3
        + [pltpu.VMEM(a.shape, a.dtype) for a in (raw_tiles, flat_profile, dark_profile)]
        + [pltpu.SMEM((slots,), jnp.int32)] * 3
        + [pltpu.SemaphoreType.DMA((6,))],
        compiler_params=grant(4),
        name="pack",
    )(
        *[
            pltpu.with_memory_space_constraint(a, pltpu.HBM)
            for a in (destinations.reshape(1, tiles), positions, levels, raw_tiles, flat_profile, dark_profile)
        ]
    )
    own = packed[-1]
    others = []
    for s in range(1, planes):
        others.append(lax.ppermute(own, "plane", [(i, (i + s) % planes) for i in range(planes)]))
    pays = [packed[0]] + [None] * (classes - 1)
    for k in ORDER:
        pays[k] = lax.ppermute(packed[k], "tile", [(i, (i + steps[k]) % count) for i in range(count)])
    full = pltpu.VMEM((channels, rows, width), jnp.float32)
    rflat, darkf = pl.pallas_call(
        functools.partial(profile_kernel, planes, rows),
        out_shape=[full, full],
        in_specs=[vmem()] * planes,
        out_specs=[vmem()] * 2,
        compiler_params=grant(4),
        name="profile",
    )(*resident(own, *others))
    strip = pltpu.VMEM((channels * 8, width), jnp.bfloat16)
    top, bot = pl.pallas_call(
        functools.partial(strip_kernel, float(CR // rows - 1), width),
        out_shape=[strip, strip],
        in_specs=[vmem()] * (classes + 2),
        out_specs=[vmem()] * 2,
        compiler_params=grant(4),
        name="strips",
    )(*resident(*pays, rflat, darkf))
    above = lax.ppermute(bot, "tile", [(i, i + 1) for i in range(count - 1)])
    below = lax.ppermute(top, "tile", [(i + 1, i) for i in range(count - 1)])
    field, edges = pl.pallas_call(
        functools.partial(main_kernel, width),
        grid=(channels,),
        out_shape=[
            jax.ShapeDtypeStruct((1, channels, CR, width), jnp.bfloat16),
            pltpu.VMEM((channels, 16, width), jnp.float32),
        ],
        in_specs=[vmem()] * (classes + 2),
        out_specs=[
            pl.BlockSpec((1, 1, CR, width), lambda c: (0, c, 0, 0)),
            vmem(),
        ],
        scratch_shapes=[
            pltpu.VMEM((CR, classes * 128), jnp.bfloat16),
            pltpu.VMEM((classes * 128, width), jnp.bfloat16),
        ],
        compiler_params=grant(24),
        name="place",
    )(*resident(*pays, rflat, darkf))
    return pl.pallas_call(
        functools.partial(edge_kernel, count),
        out_shape=jax.ShapeDtypeStruct(field.shape, field.dtype),
        in_specs=[pl.BlockSpec(memory_space=pl.ANY)] + [vmem()] * 5,
        out_specs=pl.BlockSpec(memory_space=pl.ANY),
        scratch_shapes=[
            pltpu.VMEM((4, 16, width), jnp.bfloat16),
            pltpu.SemaphoreType.DMA((4,)),
            pltpu.SemaphoreType.DMA((4,)),
        ],
        input_output_aliases={0: 0},
        compiler_params=grant(4),
        name="edge",
    )(field, *resident(edges, above, below, top, bot))


def solution(mesh):
    placed = (
        P("plane", "tile", None, None, None),
        P(None, "plane", None),
        P(None, "plane", None),
        P("plane", "tile", None),
        P("plane", "tile"),
        P("plane", "tile"),
    )
    return jax.shard_map(
        stitch,
        mesh=mesh,
        in_specs=placed,
        out_specs=P("plane", None, "tile", None),
        check_vma=False,
    )
```
